1024 devices in a mesh: gx: 4 (over x), gy: 8 (over y, core), gz: 32 (over z).
Axes of the slice: x: 4, y: 4, z: 32, core: 2. Of those that a mesh axis runs over, the one named last changes fastest.
Arguments:
- volume: float32 [1024, 512, 1024], P('gz', 'gx', 'gy'), may hold values from -3.5 to 3.5
Outputs:
- image: float32 [4, 512, 1024], P(None, 'gx', 'gy')
The draws below stay inside these ranges and needn't reach their ends.
All inputs are finite; a program needn't handle non-finite values.
Results may differ from the reference program's by a relative error of at most 0.0003.
Values sent between devices are 32-bit elements; how exact they have to be, the bound alone decides.
No kernel may reach another device: no remote copies, remote signals or barrier semaphores. Data moves between devices by JAX's collectives and lax.ppermute only.
A program may use at most 64 MiB of HBM per device.

```python
import jax
import jax.numpy as jnp
from jax import lax

NX = 512
NY = 1024
NZ = 1024


def block_scale(own_key, shape, pieces, smallest, high):
    def one(position, shards_of):
        heights = jax.random.uniform(jax.random.fold_in(jax.random.fold_in(own_key, 6), position), (shards_of,), jnp.float32, smallest / len(pieces), high / len(pieces))
        return jnp.repeat(jnp.exp(heights), shape[position] // shards_of).reshape((-1,) + (1,) * (len(shape) - position - 1))

    factor_of = one(*pieces[0])
    for cut in pieces[1:]:
        factor_of = factor_of * one(*cut)
    return factor_of


def bell_draw(key, dims, deviation, reach, pieces=(), kind=jnp.bfloat16):
    loudness = block_scale(key, dims, pieces, -0.22, 0.18) if pieces else 1.0
    entries = jax.random.normal(key, dims, jnp.float32) * deviation * loudness
    return jnp.minimum(jnp.maximum(entries, -reach), reach).astype(kind)


def setup_inputs(seed: int = 0) -> dict:
    key_list = jax.random.split(jax.random.key(seed), 2)
    return {
        "volume": bell_draw(key_list[0], (NZ, NX, NY), 1.0, 3.5, ((0, 32), (1, 4), (2, 8)), jnp.float32),
    }


def shade_block(extended, depth_cells):
    centre = extended[1:-1, 1:-1, 1:-1]
    slope_z = 0.5 * (extended[2:, 1:-1, 1:-1] - extended[:-2, 1:-1, 1:-1])
    slope_x = 0.5 * (extended[1:-1, 2:, 1:-1] - extended[1:-1, :-2, 1:-1])
    slope_y = 0.5 * (extended[1:-1, 1:-1, 2:] - extended[1:-1, 1:-1, :-2])
    facing = (2.0 * slope_z + slope_x + 2.0 * slope_y) / 3.0
    length = jnp.sqrt(slope_z * slope_z + slope_x * slope_x + slope_y * slope_y + 1.0)
    shading = 0.2 + 2.0 * jnp.abs(facing) / length
    thickness = 2.0 * jnp.exp(centre) / depth_cells
    opacity = -jnp.expm1(-thickness)
    weighted = shading * opacity
    colors = jnp.stack([jax.nn.sigmoid(2.0 * centre + 1.0), jnp.exp(-centre * centre), jax.nn.sigmoid(1.0 - 2.0 * centre)]) * weighted
    return (thickness, colors)

def reference(volume):
    block_rows = 8
    count = NX // block_rows

    def render(index):
        first_row = index * block_rows
        middle = lax.dynamic_slice_in_dim(volume, first_row, block_rows, 1).astype(jnp.float32)
        lower_rim = lax.dynamic_slice_in_dim(volume, jnp.maximum(first_row - 1, 0), 1, 1).astype(jnp.float32)
        lower_rim = lower_rim * (first_row > 0).astype(jnp.float32)
        upper_rim = lax.dynamic_slice_in_dim(volume, jnp.minimum(first_row + block_rows, NX - 1), 1, 1).astype(jnp.float32)
        upper_rim = upper_rim * (first_row + block_rows < NX).astype(jnp.float32)
        rows = jnp.concatenate([lower_rim, middle, upper_rim], axis=1)
        extended = jnp.pad(rows, ((1, 1), (0, 0), (1, 1)))
        thickness, colors = shade_block(extended, NZ)
        before = jnp.cumsum(thickness, axis=0) - thickness
        picture = lax.optimization_barrier(jnp.sum(jnp.exp(-before) * colors, axis=1))
        coverage = -jnp.expm1(-lax.optimization_barrier(jnp.sum(thickness, axis=0)))
        return jnp.concatenate([picture, coverage[None]], axis=0)
    blocks = lax.map(render, jnp.arange(count, dtype=jnp.int32))
    return jnp.transpose(blocks, (1, 0, 2, 3)).reshape(4, NX, NY)
```

```python
import functools

import jax
import jax.numpy as jnp
from jax import lax
from jax.experimental import pallas as pl
from jax.experimental.pallas import tpu as pltpu
from jax.sharding import PartitionSpec as P

LOG2E = 1.4426950408889634
E = 2.718281828459045
VMEM = pltpu.VMEM


def whole():
    return pl.BlockSpec(memory_space=VMEM)


def faces_kernel(v_ref, zlo_ref, zhi_ref, xlo_ref, xhi_ref, y_ref):
    nz, nx, ny = v_ref.shape
    zlo_ref[...] = v_ref[0]
    zhi_ref[...] = v_ref[nz - 1]
    for z in range(nz):
        xlo_ref[z : z + 1, :] = v_ref[z, 0:1, :]
        xhi_ref[z : z + 1, :] = v_ref[z, nx - 1 : nx, :]
    lane_pair = lax.broadcasted_iota(jnp.int32, (8, ny), 1) // 2

    @pl.loop(0, nx // 8)
    def _(j):
        rows = pl.ds(pl.multiple_of(j * 8, 8), 8)
        packed = jnp.zeros((8, ny), jnp.float32)
        for z in range(nz):
            turned = pltpu.roll(v_ref[z, rows, :], 2 * z + 1, 1)
            packed = jnp.where(lane_pair == z, turned, packed)
        y_ref[rows, :] = packed


def faces(volume):
    nz, nx, ny = volume.shape
    plane = jax.ShapeDtypeStruct((nx, ny), jnp.float32)
    row = jax.ShapeDtypeStruct((nz, ny), jnp.float32)
    return pl.pallas_call(
        faces_kernel,
        out_shape=(plane, plane, row, row, plane),
        in_specs=[whole()],
        out_specs=[whole()] * 5,
        compiler_params=pltpu.CompilerParams(vmem_limit_bytes=8 << 20),
        cost_estimate=pl.CostEstimate(flops=1 << 20, bytes_accessed=nz * nx * ny * 4, transcendentals=0),
        name="faces",
    )(volume)


def render_kernel(scale, v_ref, zlo_ref, zhi_ref, xlo_ref, xhi_ref, ylo_ref, yhi_ref, out_ref, grid_ref, edge_ref, part_ref, sem):
    nz, nx, ny = v_ref.shape
    copy = pltpu.make_async_copy(v_ref, grid_ref.at[1 : nz + 1, 8 : nx + 8, :], sem)
    copy.start()
    lane = lax.broadcasted_iota(jnp.int32, (nx, ny), 1)
    edge_ref[...] = jnp.where(lane % 2 == 1, pltpu.roll(ylo_ref[...], 1, 1), pltpu.roll(yhi_ref[...], ny - 1, 1))
    grid_ref[0, 8 : nx + 8, :] = zlo_ref[...]
    grid_ref[nz + 1, 8 : nx + 8, :] = zhi_ref[...]
    for z in range(nz):
        grid_ref[z + 1, 7:8, :] = xlo_ref[z : z + 1, :]
        grid_ref[z + 1, nx + 8 : nx + 9, :] = xhi_ref[z : z + 1, :]
    copy.wait()
    height = 16
    col = lax.broadcasted_iota(jnp.int32, (height, ny), 1)
    first, last = col == 0, col == ny - 1

    for block in range(nx // height):
        start = block * height
        edge = edge_ref[start : start + height, :]

        def step(z, carry):
            prev, cur, clear, red, green, blue = carry
            new = grid_ref[z + 2, start + 8 : start + 8 + height, :]
            above = grid_ref[z + 1, start + 7 : start + 7 + height, :]
            below = grid_ref[z + 1, start + 9 : start + 9 + height, :]
            outer = pltpu.roll(edge, ny - 1 - 2 * z, 1)
            left = jnp.where(first, outer, pltpu.roll(cur, 1, 1))
            right = jnp.where(last, outer, pltpu.roll(cur, ny - 1, 1))
            dz = new - prev
            dx = below - above
            dy = right - left
            facing = jnp.abs(2.0 * (dz + dy) + dx)
            shading = 0.2 + (2.0 / 3.0) * facing * lax.rsqrt(dz * dz + dx * dx + dy * dy + 4.0)
            grown = jnp.exp(cur)
            thick = grown * scale
            opacity = thick * (1.0 + thick * (-1.0 / 2 + thick * (1.0 / 6 + thick * (-1.0 / 24 + thick * (1.0 / 120)))))
            square = grown * grown
            up = square * E
            low = 1.0 + square * (1.0 / E)
            ratio = 1.0 / ((1.0 + up) * low)
            weight = clear * opacity
            lit = weight * shading
            red = red + lit * (up * low * ratio)
            green = green + lit * jnp.exp(-cur * cur)
            blue = blue + lit * ((1.0 + up) * ratio)
            return (cur, new, clear - weight, red, green, blue)

        zero = jnp.zeros((height, ny), jnp.float32)
        carry = (
            grid_ref[0, start + 8 : start + 8 + height, :],
            grid_ref[1, start + 8 : start + 8 + height, :],
            zero + 1.0,
            zero,
            zero,
            zero,
        )
        carry = lax.fori_loop(0, nz, step, carry, unroll=4)
        _, _, clear, red, green, blue = carry
        for c, value in enumerate((red, green, blue, clear)):
            part_ref[c, start : start + height, :] = value
    chunk = out_ref.shape[1] // 4
    for k in range(out_ref.shape[0]):
        for c in range(4):
            out_ref[k, c * chunk : (c + 1) * chunk, :] = part_ref[c, k * chunk : (k + 1) * chunk, :]


def render(volume, halo, depth_cells, pieces):
    nz, nx, ny = volume.shape
    return pl.pallas_call(
        functools.partial(render_kernel, 2.0 / depth_cells),
        out_shape=jax.ShapeDtypeStruct((pieces, 4 * nx // pieces, ny), jnp.float32),
        in_specs=[pl.BlockSpec(memory_space=pl.ANY)] + [whole()] * 6,
        out_specs=whole(),
        scratch_shapes=[
            VMEM((nz + 2, nx + 16, ny), jnp.float32),
            VMEM((nx, ny), jnp.float32),
            VMEM((4, nx, ny), jnp.float32),
            pltpu.SemaphoreType.DMA,
        ],
        compiler_params=pltpu.CompilerParams(vmem_limit_bytes=16 << 20),
        name="render",
    )(volume, *halo)


def merge_kernel(parts_ref, out_ref):
    count, rows, ny = parts_ref.shape
    part = rows // 4
    shape = (part, ny)
    clear = jnp.ones(shape, jnp.float32)
    total = [jnp.zeros(shape, jnp.float32) for _ in range(3)]
    for k in range(count):
        for c in range(3):
            total[c] = total[c] + clear * parts_ref[k, c * part : (c + 1) * part, :]
        clear = clear * parts_ref[k, 3 * part :, :]
    total.append(1.0 - clear)
    for k in range(out_ref.shape[0]):
        for c in range(4):
            out_ref[k, c * part : (c + 1) * part, :] = total[c]


def merge(parts, copies):
    _, rows, ny = parts.shape
    return pl.pallas_call(
        merge_kernel,
        out_shape=jax.ShapeDtypeStruct((copies, rows, ny), jnp.float32),
        in_specs=[whole()],
        out_specs=whole(),
        compiler_params=pltpu.CompilerParams(vmem_limit_bytes=8 << 20),
        name="merge",
    )(parts)


def lay_kernel(parts_ref, out_ref):
    count, rows, ny = parts_ref.shape
    part = rows // 4
    for k in range(count):
        for c in range(4):
            out_ref[c, k * part : (k + 1) * part, :] = parts_ref[k, c * part : (c + 1) * part, :]


def lay(parts):
    count, rows, ny = parts.shape
    return pl.pallas_call(
        lay_kernel,
        out_shape=jax.ShapeDtypeStruct((4, count * rows // 4, ny), jnp.float32),
        in_specs=[whole()],
        out_specs=whole(),
        compiler_params=pltpu.CompilerParams(vmem_limit_bytes=8 << 20),
        name="lay",
    )(parts)


def shift(array, axis, upward):
    devices = lax.axis_size(axis)
    pairs = [(i, i + 1) if upward else (i + 1, i) for i in range(devices - 1)]
    return lax.ppermute(array, axis, pairs)


def per_device(volume):
    bricks = lax.axis_size("gz")
    depth_cells = volume.shape[0] * bricks
    zlo, zhi, xlo, xhi, y = faces(volume)
    halo = (
        shift(zhi, "gz", True),
        shift(zlo, "gz", False),
        shift(xhi, "gx", True),
        shift(xlo, "gx", False),
        shift(y, "gy", True),
        shift(y, "gy", False),
    )
    parts = render(volume, halo, depth_cells, bricks)
    parts = lax.all_to_all(parts, "gz", 0, 0)
    merged = merge(parts, bricks)
    return lay(lax.all_to_all(merged, "gz", 0, 0))


def solution(mesh):
    return jax.shard_map(
        per_device,
        mesh=mesh,
        in_specs=(P("gz", "gx", "gy"),),
        out_specs=P(None, "gx", "gy"),
        check_vma=False,
    )
```

```python
import functools

import jax
import jax.numpy as jnp
from jax import lax
from jax.experimental import pallas as pl
from jax.experimental.pallas import tpu as pltpu
from jax.sharding import PartitionSpec as P

LOG2E = 1.4426950408889634
E = 2.718281828459045
VMEM = pltpu.VMEM


def whole():
    return pl.BlockSpec(memory_space=VMEM)


def faces_kernel(v_ref, zlo_ref, zhi_ref, xlo_ref, xhi_ref, y_ref):
    nz, nx, ny = v_ref.shape
    zlo_ref[...] = v_ref[0]
    zhi_ref[...] = v_ref[nz - 1]
    for z in range(nz):
        xlo_ref[z : z + 1, :] = v_ref[z, 0:1, :]
        xhi_ref[z : z + 1, :] = v_ref[z, nx - 1 : nx, :]
    lane_pair = lax.broadcasted_iota(jnp.int32, (8, ny), 1) // 2

    @pl.loop(0, nx // 8)
    def _(j):
        rows = pl.ds(pl.multiple_of(j * 8, 8), 8)
        packed = jnp.zeros((8, ny), jnp.float32)
        for z in range(nz):
            turned = pltpu.roll(v_ref[z, rows, :], 2 * z + 1, 1)
            packed = jnp.where(lane_pair == z, turned, packed)
        y_ref[rows, :] = packed


def faces(volume):
    nz, nx, ny = volume.shape
    plane = jax.ShapeDtypeStruct((nx, ny), jnp.float32)
    row = jax.ShapeDtypeStruct((nz, ny), jnp.float32)
    return pl.pallas_call(
        faces_kernel,
        out_shape=(plane, plane, row, row, plane),
        in_specs=[whole()],
        out_specs=[whole()] * 5,
        compiler_params=pltpu.CompilerParams(vmem_limit_bytes=8 << 20),
        cost_estimate=pl.CostEstimate(flops=1 << 20, bytes_accessed=nz * nx * ny * 4, transcendentals=0),
        name="faces",
    )(volume)


def render_kernel(scale, v_ref, zlo_ref, zhi_ref, xlo_ref, xhi_ref, ylo_ref, yhi_ref, out_ref, grid_ref, edge_ref, sem):
    nz, nx, ny = v_ref.shape
    copy = pltpu.make_async_copy(v_ref, grid_ref.at[1 : nz + 1, 8 : nx + 8, :], sem)
    copy.start()
    lane = lax.broadcasted_iota(jnp.int32, (nx, ny), 1)
    edge_ref[...] = jnp.where(lane % 2 == 1, pltpu.roll(ylo_ref[...], 1, 1), pltpu.roll(yhi_ref[...], ny - 1, 1))
    grid_ref[0, 8 : nx + 8, :] = zlo_ref[...]
    grid_ref[nz + 1, 8 : nx + 8, :] = zhi_ref[...]
    for z in range(nz):
        grid_ref[z + 1, 7:8, :] = xlo_ref[z : z + 1, :]
        grid_ref[z + 1, nx + 8 : nx + 9, :] = xhi_ref[z : z + 1, :]
    copy.wait()
    height = nx // out_ref.shape[0]
    col = lax.broadcasted_iota(jnp.int32, (height, ny), 1)
    first, last = col == 0, col == ny - 1

    for block in range(nx // height):
        start = block * height
        edge = edge_ref[start : start + height, :]

        def step(z, carry):
            prev, cur, clear, red, green, blue = carry
            new = grid_ref[z + 2, start + 8 : start + 8 + height, :]
            above = grid_ref[z + 1, start + 7 : start + 7 + height, :]
            below = grid_ref[z + 1, start + 9 : start + 9 + height, :]
            outer = pltpu.roll(edge, ny - 1 - 2 * z, 1)
            left = jnp.where(first, outer, pltpu.roll(cur, 1, 1))
            right = jnp.where(last, outer, pltpu.roll(cur, ny - 1, 1))
            dz = new - prev
            dx = below - above
            dy = right - left
            facing = jnp.abs(2.0 * (dz + dy) + dx)
            shading = 0.2 + (2.0 / 3.0) * facing * lax.rsqrt(dz * dz + dx * dx + dy * dy + 4.0)
            grown = jnp.exp(cur)
            thick = grown * scale
            opacity = thick * (1.0 + thick * (-1.0 / 2 + thick * (1.0 / 6 + thick * (-1.0 / 24 + thick * (1.0 / 120)))))
            square = grown * grown
            up = square * E
            low = 1.0 + square * (1.0 / E)
            ratio = 1.0 / ((1.0 + up) * low)
            weight = clear * opacity
            lit = weight * shading
            red = red + lit * (up * low * ratio)
            green = green + lit * jnp.exp(-cur * cur)
            blue = blue + lit * ((1.0 + up) * ratio)
            return (cur, new, clear - weight, red, green, blue)

        zero = jnp.zeros((height, ny), jnp.float32)
        carry = (
            grid_ref[0, start + 8 : start + 8 + height, :],
            grid_ref[1, start + 8 : start + 8 + height, :],
            zero + 1.0,
            zero,
            zero,
            zero,
        )
        carry = lax.fori_loop(0, nz, step, carry, unroll=4)
        _, _, clear, red, green, blue = carry
        for c, value in enumerate((red, green, blue, clear)):
            out_ref[block, c * height : (c + 1) * height, :] = value


def render(volume, halo, depth_cells, pieces):
    nz, nx, ny = volume.shape
    return pl.pallas_call(
        functools.partial(render_kernel, 2.0 / depth_cells),
        out_shape=jax.ShapeDtypeStruct((pieces, 4 * nx // pieces, ny), jnp.float32),
        in_specs=[pl.BlockSpec(memory_space=pl.ANY)] + [whole()] * 6,
        out_specs=whole(),
        scratch_shapes=[
            VMEM((nz + 2, nx + 16, ny), jnp.float32),
            VMEM((nx, ny), jnp.float32),
            pltpu.SemaphoreType.DMA,
        ],
        compiler_params=pltpu.CompilerParams(vmem_limit_bytes=16 << 20),
        name="render",
    )(volume, *halo)


def merge_kernel(final, parts_ref, out_ref):
    count, rows, ny = parts_ref.shape
    part = rows // 4
    clear = parts_ref[0, 3 * part :, :]
    total = [parts_ref[0, c * part : (c + 1) * part, :] for c in range(3)]
    for k in range(1, count):
        for c in range(3):
            total[c] = total[c] + clear * parts_ref[k, c * part : (c + 1) * part, :]
        clear = clear * parts_ref[k, 3 * part :, :]
    total.append(1.0 - clear if final else clear)
    for k in range(out_ref.shape[0]):
        for c in range(4):
            out_ref[k, c * part : (c + 1) * part, :] = total[c]


def merge(parts, copies, final):
    _, rows, ny = parts.shape
    return pl.pallas_call(
        functools.partial(merge_kernel, final),
        out_shape=jax.ShapeDtypeStruct((copies, rows, ny), jnp.float32),
        in_specs=[whole()],
        out_specs=whole(),
        compiler_params=pltpu.CompilerParams(vmem_limit_bytes=8 << 20),
        name="merge",
    )(parts)


def lay_kernel(parts_ref, out_ref):
    count, rows, ny = parts_ref.shape
    part = rows // 4
    for k in range(count):
        for c in range(4):
            out_ref[c, k * part : (k + 1) * part, :] = parts_ref[k, c * part : (c + 1) * part, :]


def lay(parts):
    count, rows, ny = parts.shape
    return pl.pallas_call(
        lay_kernel,
        out_shape=jax.ShapeDtypeStruct((4, count * rows // 4, ny), jnp.float32),
        in_specs=[whole()],
        out_specs=whole(),
        compiler_params=pltpu.CompilerParams(vmem_limit_bytes=8 << 20),
        name="lay",
    )(parts)


def shift(array, axis, upward):
    devices = lax.axis_size(axis)
    pairs = [(i, i + 1) if upward else (i + 1, i) for i in range(devices - 1)]
    return lax.ppermute(array, axis, pairs)


def per_device(volume):
    bricks = lax.axis_size("gz")
    depth_cells = volume.shape[0] * bricks
    zlo, zhi, xlo, xhi, y = faces(volume)
    halo = (
        shift(zhi, "gz", True),
        shift(zlo, "gz", False),
        shift(xhi, "gx", True),
        shift(xlo, "gx", False),
        shift(y, "gy", True),
        shift(y, "gy", False),
    )
    near = max(n for n in (1, 2, 4, 8) if bricks % n == 0)
    far = bricks // near
    runs = [[g * near + i for i in range(near)] for g in range(far)]
    strides = [[g * near + i for g in range(far)] for i in range(near)]
    parts = render(volume, halo, depth_cells, near)
    parts = lax.all_to_all(parts, "gz", 0, 0, axis_index_groups=runs)
    parts = merge(parts, far, False)
    parts = lax.all_to_all(parts, "gz", 0, 0, axis_index_groups=strides)
    parts = merge(parts, near, True)
    return lay(lax.all_to_all(parts, "gz", 0, 0, axis_index_groups=runs))


def solution(mesh):
    return jax.shard_map(
        per_device,
        mesh=mesh,
        in_specs=(P("gz", "gx", "gy"),),
        out_specs=P(None, "gx", "gy"),
        check_vma=False,
    )
```

```python
import functools

import jax
import jax.numpy as jnp
from jax import lax
from jax.experimental import pallas as pl
from jax.experimental.pallas import tpu as pltpu
from jax.sharding import PartitionSpec as P

E = 2.718281828459045
VMEM = pltpu.VMEM


def whole():
    return pl.BlockSpec(memory_space=VMEM)


def faces_kernel(steps, v_ref, own_ref, zlo_ref, zhi_ref, xlo_ref, xhi_ref, y_ref, sems):
    nz, nx, ny = v_ref.shape
    deep = nz // steps
    copies = []
    for i in range(steps):
        planes = slice(i * deep, (i + 1) * deep)
        copies.append(pltpu.make_async_copy(v_ref.at[planes], own_ref.at[planes], sems.at[i]))
        copies[-1].start()
    lane_pair = lax.broadcasted_iota(jnp.int32, (8, ny), 1) // 2
    for i in range(steps):
        copies[i].wait()
        for row in range(0, nx, 8):
            packed = jnp.zeros((8, ny), jnp.float32) if i == 0 else y_ref[row : row + 8, :]
            for z in range(i * deep, (i + 1) * deep):
                turned = pltpu.roll(own_ref[z, row : row + 8, :], 2 * z + 1, 1)
                packed = jnp.where(lane_pair == z, turned, packed)
            y_ref[row : row + 8, :] = packed
        for z in range(i * deep, (i + 1) * deep):
            xlo_ref[z : z + 1, :] = own_ref[z, 0:1, :]
            xhi_ref[z : z + 1, :] = own_ref[z, nx - 1 : nx, :]
    zlo_ref[...] = own_ref[0]
    zhi_ref[...] = own_ref[nz - 1]


def faces(volume):
    nz, nx, ny = volume.shape
    steps = 4
    plane = jax.ShapeDtypeStruct((nx, ny), jnp.float32)
    row = jax.ShapeDtypeStruct((nz, ny), jnp.float32)
    return pl.pallas_call(
        functools.partial(faces_kernel, steps),
        out_shape=(jax.ShapeDtypeStruct(volume.shape, jnp.float32), plane, plane, row, row, plane),
        in_specs=[pl.BlockSpec(memory_space=pltpu.HBM)],
        out_specs=[whole()] * 6,
        scratch_shapes=[pltpu.SemaphoreType.DMA((steps,))],
        compiler_params=pltpu.CompilerParams(vmem_limit_bytes=8 << 20),
        name="faces",
    )(pltpu.with_memory_space_constraint(volume, pltpu.HBM))


def weigh_kernel(scale, v_ref, red_ref, green_ref, blue_ref, clear_ref):
    nz, nx, ny = v_ref.shape
    height, unroll = 16, 16
    for start in range(0, nx, height):
        rows = slice(start, start + height)

        def group(k, clear):
            for i in range(unroll):
                z = k * unroll + i
                cur = v_ref[z, rows, :]
                grown = jnp.exp(cur)
                thick = grown * scale
                opacity = thick * (1.0 + thick * (-1.0 / 2 + thick * (1.0 / 6 + thick * (-1.0 / 24 + thick * (1.0 / 120)))))
                square = grown * grown
                up = square * E
                low = 1.0 + square * (1.0 / E)
                ratio = 1.0 / ((1.0 + up) * low)
                weight = clear * opacity
                share = weight * ratio
                red_ref[z, rows, :] = share * (up * low)
                green_ref[z, rows, :] = weight * jnp.exp(-cur * cur)
                blue_ref[z, rows, :] = share * (1.0 + up)
                clear = clear - weight
            return clear

        clear_ref[rows, :] = lax.fori_loop(0, nz // unroll, group, jnp.ones((height, ny), jnp.float32))


def weigh(volume, depth_cells):
    nz, nx, ny = volume.shape
    brick = jax.ShapeDtypeStruct(volume.shape, jnp.float32)
    return pl.pallas_call(
        functools.partial(weigh_kernel, 2.0 / depth_cells),
        out_shape=(brick, brick, brick, jax.ShapeDtypeStruct((nx, ny), jnp.float32)),
        in_specs=[whole()],
        out_specs=[whole()] * 4,
        compiler_params=pltpu.CompilerParams(vmem_limit_bytes=12 << 20),
        cost_estimate=pl.CostEstimate(flops=30 * nz * nx * ny, bytes_accessed=16 * nz * nx * ny, transcendentals=3 * nz * nx * ny),
        name="weigh",
    )(volume)


def shade_kernel(v_ref, red_ref, green_ref, blue_ref, clear_ref, zlo_ref, zhi_ref, xlo_ref, xhi_ref, ylo_ref, yhi_ref, out_ref):
    nz, nx, ny = v_ref.shape
    pieces = out_ref.shape[0]
    height, unroll = nx // pieces, 16
    col = lax.broadcasted_iota(jnp.int32, (height, ny), 1)
    line = lax.broadcasted_iota(jnp.int32, (height, ny), 0)
    odd = col % 2 == 1
    for block in range(pieces):
        start = block * height
        rows = slice(start, start + height)
        edge = jnp.where(odd, pltpu.roll(ylo_ref[rows, :], 1, 1), pltpu.roll(yhi_ref[rows, :], ny - 1, 1))

        def step(z, prev, cur, new, sums):
            if block == 0:
                above = jnp.where(line == 0, xlo_ref[pl.ds(z, 1), :], pltpu.roll(cur, 1, 0))
            else:
                above = v_ref[z, start - 1 : start - 1 + height, :]
            if block == pieces - 1:
                below = jnp.where(line == height - 1, xhi_ref[pl.ds(z, 1), :], pltpu.roll(cur, height - 1, 0))
            else:
                below = v_ref[z, start + 1 : start + 1 + height, :]
            outer = pltpu.roll(edge, ny - 1 - 2 * z, 1)
            left = jnp.where(col == 0, outer, pltpu.roll(cur, 1, 1))
            right = jnp.where(col == ny - 1, outer, pltpu.roll(cur, ny - 1, 1))
            dz = new - prev
            dx = below - above
            dy = right - left
            facing = jnp.abs(2.0 * (dz + dy) + dx)
            shading = 0.2 + (2.0 / 3.0) * facing * lax.rsqrt(dz * dz + dx * dx + dy * dy + 4.0)
            return tuple(s + ref[z, rows, :] * shading for s, ref in zip(sums, (red_ref, green_ref, blue_ref)))

        def group(k, carry):
            prev, cur, sums = carry
            for i in range(unroll):
                z = k * unroll + i
                new = v_ref[z + 1, rows, :]
                sums = step(z, prev, cur, new, sums)
                prev, cur = cur, new
            return prev, cur, sums

        zero = jnp.zeros((height, ny), jnp.float32)
        prev, cur, sums = lax.fori_loop(0, nz // unroll - 1, group, (zlo_ref[rows, :], v_ref[0, rows, :], (zero,) * 3))
        for z in range(nz - unroll, nz):
            new = v_ref[z + 1, rows, :] if z + 1 < nz else zhi_ref[rows, :]
            sums = step(z, prev, cur, new, sums)
            prev, cur = cur, new
        for c, value in enumerate((*sums, clear_ref[rows, :])):
            out_ref[block, c * height : (c + 1) * height, :] = value


def shade(volume, weights, halo, pieces):
    nz, nx, ny = volume.shape
    return pl.pallas_call(
        shade_kernel,
        out_shape=jax.ShapeDtypeStruct((pieces, 4 * nx // pieces, ny), jnp.float32),
        in_specs=[whole()] * 11,
        out_specs=whole(),
        compiler_params=pltpu.CompilerParams(vmem_limit_bytes=12 << 20),
        name="shade",
    )(volume, *weights, *halo)


def merge_kernel(final, parts_ref, out_ref):
    count, rows, ny = parts_ref.shape
    part = rows // 4
    clear = parts_ref[0, 3 * part :, :]
    total = [parts_ref[0, c * part : (c + 1) * part, :] for c in range(3)]
    for k in range(1, count):
        for c in range(3):
            total[c] = total[c] + clear * parts_ref[k, c * part : (c + 1) * part, :]
        clear = clear * parts_ref[k, 3 * part :, :]
    total.append(1.0 - clear if final else clear)
    for k in range(out_ref.shape[0]):
        for c in range(4):
            out_ref[k, c * part : (c + 1) * part, :] = total[c]


def merge(parts, copies, final):
    _, rows, ny = parts.shape
    return pl.pallas_call(
        functools.partial(merge_kernel, final),
        out_shape=jax.ShapeDtypeStruct((copies, rows, ny), jnp.float32),
        in_specs=[whole()],
        out_specs=whole(),
        compiler_params=pltpu.CompilerParams(vmem_limit_bytes=8 << 20),
        name="merge",
    )(parts)


def lay_kernel(parts_ref, out_ref):
    count, rows, ny = parts_ref.shape
    part = rows // 4
    for k in range(count):
        for c in range(4):
            out_ref[c, k * part : (k + 1) * part, :] = parts_ref[k, c * part : (c + 1) * part, :]


def lay(parts):
    count, rows, ny = parts.shape
    return pl.pallas_call(
        lay_kernel,
        out_shape=jax.ShapeDtypeStruct((4, count * rows // 4, ny), jnp.float32),
        in_specs=[whole()],
        out_specs=whole(),
        compiler_params=pltpu.CompilerParams(vmem_limit_bytes=8 << 20),
        name="lay",
    )(parts)


def shift(array, axis, upward):
    devices = lax.axis_size(axis)
    pairs = [(i, i + 1) if upward else (i + 1, i) for i in range(devices - 1)]
    return lax.ppermute(array, axis, pairs)


def per_device(volume):
    bricks = lax.axis_size("gz")
    depth_cells = volume.shape[0] * bricks
    own, zlo, zhi, xlo, xhi, y = faces(volume)
    front = shift(zhi, "gz", True)
    back = shift(zlo, "gz", False)
    first = shift(y, "gy", True)
    last = shift(y, "gy", False)
    above = shift(xhi, "gx", True)
    xlo, front = lax.optimization_barrier((xlo, front))
    below = shift(xlo, "gx", False)
    halo = (front, back, above, below, first, last)
    near = max(n for n in (1, 2, 4, 8) if bricks % n == 0)
    far = bricks // near
    runs = [[g * near + i for i in range(near)] for g in range(far)]
    strides = [[g * near + i for g in range(far)] for i in range(near)]
    parts = shade(own, weigh(own, depth_cells), halo, near)
    parts = lax.all_to_all(parts, "gz", 0, 0, axis_index_groups=runs)
    parts = merge(parts, far, False)
    parts = lax.all_to_all(parts, "gz", 0, 0, axis_index_groups=strides)
    parts = merge(parts, near, True)
    return lay(lax.all_to_all(parts, "gz", 0, 0, axis_index_groups=runs))


def solution(mesh):
    return jax.shard_map(
        per_device,
        mesh=mesh,
        in_specs=(P("gz", "gx", "gy"),),
        out_specs=P(None, "gx", "gy"),
        check_vma=False,
    )
```

```python
import functools

import jax
import jax.numpy as jnp
from jax import lax
from jax.experimental import pallas as pl
from jax.experimental.pallas import tpu as pltpu
from jax.sharding import PartitionSpec as P

E = 2.718281828459045
VMEM = pltpu.VMEM


def whole():
    return pl.BlockSpec(memory_space=VMEM)


def faces_kernel(steps, v_ref, own_ref, zlo_ref, zhi_ref, xlo_ref, xhi_ref, y_ref, sems):
    nz, nx, ny = v_ref.shape
    deep = nz // steps
    copies = []
    for i in range(steps):
        planes = slice(i * deep, (i + 1) * deep)
        copies.append(pltpu.make_async_copy(v_ref.at[planes], own_ref.at[planes], sems.at[i]))
        copies[-1].start()
    lane_pair = lax.broadcasted_iota(jnp.int32, (8, ny), 1) // 2
    for i in range(steps):
        copies[i].wait()
        for row in range(0, nx, 8):
            packed = jnp.zeros((8, ny), jnp.float32) if i == 0 else y_ref[row : row + 8, :]
            for z in range(i * deep, (i + 1) * deep):
                turned = pltpu.roll(own_ref[z, row : row + 8, :], 2 * z + 1, 1)
                packed = jnp.where(lane_pair == z, turned, packed)
            y_ref[row : row + 8, :] = packed
        for z in range(i * deep, (i + 1) * deep):
            xlo_ref[z : z + 1, :] = own_ref[z, 0:1, :]
            xhi_ref[z : z + 1, :] = own_ref[z, nx - 1 : nx, :]
    zlo_ref[...] = own_ref[0]
    zhi_ref[...] = own_ref[nz - 1]


def faces(volume):
    nz, nx, ny = volume.shape
    steps = 4
    plane = jax.ShapeDtypeStruct((nx, ny), jnp.float32)
    row = jax.ShapeDtypeStruct((nz, ny), jnp.float32)
    return pl.pallas_call(
        functools.partial(faces_kernel, steps),
        out_shape=(jax.ShapeDtypeStruct(volume.shape, jnp.float32), plane, plane, row, row, plane),
        in_specs=[pl.BlockSpec(memory_space=pltpu.HBM)],
        out_specs=[whole()] * 6,
        scratch_shapes=[pltpu.SemaphoreType.DMA((steps,))],
        compiler_params=pltpu.CompilerParams(vmem_limit_bytes=8 << 20),
        name="faces",
    )(pltpu.with_memory_space_constraint(volume, pltpu.HBM))


def weigh_kernel(scale, v_ref, red_ref, green_ref, blue_ref, clear_ref):
    nz, nx, ny = v_ref.shape
    height, unroll = 16, 16
    for start in range(0, nx, height):
        rows = slice(start, start + height)

        def group(k, clear):
            for i in range(unroll):
                z = k * unroll + i
                cur = v_ref[z, rows, :]
                grown = jnp.exp(cur)
                thick = grown * scale
                opacity = thick * (1.0 + thick * (-1.0 / 2 + thick * (1.0 / 6 + thick * (-1.0 / 24 + thick * (1.0 / 120)))))
                square = grown * grown
                up = square * E
                low = 1.0 + square * (1.0 / E)
                ratio = 1.0 / ((1.0 + up) * low)
                weight = clear * opacity
                share = weight * ratio
                red_ref[z, rows, :] = share * (up * low)
                green_ref[z, rows, :] = weight * jnp.exp(-cur * cur)
                blue_ref[z, rows, :] = share * (1.0 + up)
                clear = clear - weight
            return clear

        clear_ref[rows, :] = lax.fori_loop(0, nz // unroll, group, jnp.ones((height, ny), jnp.float32))


def weigh(volume, depth_cells):
    nz, nx, ny = volume.shape
    brick = jax.ShapeDtypeStruct(volume.shape, jnp.float32)
    return pl.pallas_call(
        functools.partial(weigh_kernel, 2.0 / depth_cells),
        out_shape=(brick, brick, brick, jax.ShapeDtypeStruct((nx, ny), jnp.float32)),
        in_specs=[whole()],
        out_specs=[whole()] * 4,
        compiler_params=pltpu.CompilerParams(vmem_limit_bytes=12 << 20),
        cost_estimate=pl.CostEstimate(flops=30 * nz * nx * ny, bytes_accessed=16 * nz * nx * ny, transcendentals=3 * nz * nx * ny),
        name="weigh",
    )(volume)


def shade_rows(v_ref, weight_refs, clear_ref, zlo_ref, zhi_ref, ylo_ref, yhi_ref, out_ref, block, xlo_ref=None, xhi_ref=None):
    nz, nx, ny = v_ref.shape
    height, unroll = nx // out_ref.shape[0], 16
    col = lax.broadcasted_iota(jnp.int32, (height, ny), 1)
    line = lax.broadcasted_iota(jnp.int32, (height, ny), 0)
    start = block * height
    rows = slice(start, start + height)
    edge = jnp.where(col % 2 == 1, pltpu.roll(ylo_ref[rows, :], 1, 1), pltpu.roll(yhi_ref[rows, :], ny - 1, 1))

    def step(z, prev, cur, new, sums):
        if start == 0:
            above = jnp.where(line == 0, xlo_ref[pl.ds(z, 1), :], pltpu.roll(cur, 1, 0))
        else:
            above = v_ref[z, start - 1 : start - 1 + height, :]
        if start + height == nx:
            below = jnp.where(line == height - 1, xhi_ref[pl.ds(z, 1), :], pltpu.roll(cur, height - 1, 0))
        else:
            below = v_ref[z, start + 1 : start + 1 + height, :]
        outer = pltpu.roll(edge, ny - 1 - 2 * z, 1)
        left = jnp.where(col == 0, outer, pltpu.roll(cur, 1, 1))
        right = jnp.where(col == ny - 1, outer, pltpu.roll(cur, ny - 1, 1))
        dz = new - prev
        dx = below - above
        dy = right - left
        facing = jnp.abs(2.0 * (dz + dy) + dx)
        shading = 0.2 + (2.0 / 3.0) * facing * lax.rsqrt(dz * dz + dx * dx + dy * dy + 4.0)
        return tuple(s + ref[z, rows, :] * shading for s, ref in zip(sums, weight_refs))

    def group(k, carry):
        prev, cur, sums = carry
        for i in range(unroll):
            z = k * unroll + i
            new = v_ref[z + 1, rows, :]
            sums = step(z, prev, cur, new, sums)
            prev, cur = cur, new
        return prev, cur, sums

    zero = jnp.zeros((height, ny), jnp.float32)
    prev, cur, sums = lax.fori_loop(0, nz // unroll - 1, group, (zlo_ref[rows, :], v_ref[0, rows, :], (zero,) * 3))
    for z in range(nz - unroll, nz):
        new = v_ref[z + 1, rows, :] if z + 1 < nz else zhi_ref[rows, :]
        sums = step(z, prev, cur, new, sums)
        prev, cur = cur, new
    for c, value in enumerate((*sums, clear_ref[rows, :])):
        out_ref[block, c * height : (c + 1) * height, :] = value


def inner_kernel(v_ref, red_ref, green_ref, blue_ref, clear_ref, zlo_ref, zhi_ref, ylo_ref, yhi_ref, out_ref):
    for block in range(1, out_ref.shape[0] - 1):
        shade_rows(v_ref, (red_ref, green_ref, blue_ref), clear_ref, zlo_ref, zhi_ref, ylo_ref, yhi_ref, out_ref, block)


def outer_kernel(v_ref, red_ref, green_ref, blue_ref, clear_ref, zlo_ref, zhi_ref, ylo_ref, yhi_ref, xlo_ref, xhi_ref, inner_ref, out_ref):
    pieces = out_ref.shape[0]
    out_ref[1 : pieces - 1] = inner_ref[1 : pieces - 1]
    for block in (0, pieces - 1):
        shade_rows(v_ref, (red_ref, green_ref, blue_ref), clear_ref, zlo_ref, zhi_ref, ylo_ref, yhi_ref, out_ref, block, xlo_ref, xhi_ref)


def shade(volume, weights, halo, pieces):
    nz, nx, ny = volume.shape
    out = jax.ShapeDtypeStruct((pieces, 4 * nx // pieces, ny), jnp.float32)
    front, back, above, below, first, last = halo
    cells = nz * nx * ny
    inner = pl.pallas_call(
        inner_kernel,
        out_shape=out,
        in_specs=[whole()] * 9,
        out_specs=whole(),
        compiler_params=pltpu.CompilerParams(vmem_limit_bytes=12 << 20),
        cost_estimate=pl.CostEstimate(flops=30 * cells, bytes_accessed=16 * cells, transcendentals=cells),
        name="shade_inner",
    )(volume, *weights, front, back, first, last)
    return pl.pallas_call(
        outer_kernel,
        out_shape=out,
        in_specs=[whole()] * 12,
        out_specs=whole(),
        compiler_params=pltpu.CompilerParams(vmem_limit_bytes=12 << 20),
        name="shade_outer",
    )(volume, *weights, front, back, first, last, above, below, inner)


def merge_kernel(final, parts_ref, out_ref):
    count, rows, ny = parts_ref.shape
    part = rows // 4
    clear = parts_ref[0, 3 * part :, :]
    total = [parts_ref[0, c * part : (c + 1) * part, :] for c in range(3)]
    for k in range(1, count):
        for c in range(3):
            total[c] = total[c] + clear * parts_ref[k, c * part : (c + 1) * part, :]
        clear = clear * parts_ref[k, 3 * part :, :]
    total.append(1.0 - clear if final else clear)
    for k in range(out_ref.shape[0]):
        for c in range(4):
            out_ref[k, c * part : (c + 1) * part, :] = total[c]


def merge(parts, copies, final):
    _, rows, ny = parts.shape
    return pl.pallas_call(
        functools.partial(merge_kernel, final),
        out_shape=jax.ShapeDtypeStruct((copies, rows, ny), jnp.float32),
        in_specs=[whole()],
        out_specs=whole(),
        compiler_params=pltpu.CompilerParams(vmem_limit_bytes=8 << 20),
        name="merge",
    )(parts)


def lay_kernel(parts_ref, out_ref):
    count, rows, ny = parts_ref.shape
    part = rows // 4
    for k in range(count):
        for c in range(4):
            out_ref[c, k * part : (k + 1) * part, :] = parts_ref[k, c * part : (c + 1) * part, :]


def lay(parts):
    count, rows, ny = parts.shape
    return pl.pallas_call(
        lay_kernel,
        out_shape=jax.ShapeDtypeStruct((4, count * rows // 4, ny), jnp.float32),
        in_specs=[whole()],
        out_specs=whole(),
        compiler_params=pltpu.CompilerParams(vmem_limit_bytes=8 << 20),
        name="lay",
    )(parts)


def shift(array, axis, upward):
    devices = lax.axis_size(axis)
    pairs = [(i, i + 1) if upward else (i + 1, i) for i in range(devices - 1)]
    return lax.ppermute(array, axis, pairs)


def per_device(volume):
    bricks = lax.axis_size("gz")
    depth_cells = volume.shape[0] * bricks
    own, zlo, zhi, xlo, xhi, y = faces(volume)
    front = shift(zhi, "gz", True)
    back = shift(zlo, "gz", False)
    first = shift(y, "gy", True)
    last = shift(y, "gy", False)
    above = shift(xhi, "gx", True)
    xlo, front = lax.optimization_barrier((xlo, front))
    below = shift(xlo, "gx", False)
    halo = (front, back, above, below, first, last)
    near = max(n for n in (1, 2, 4, 8) if bricks % n == 0)
    far = bricks // near
    runs = [[g * near + i for i in range(near)] for g in range(far)]
    strides = [[g * near + i for g in range(far)] for i in range(near)]
    parts = shade(own, weigh(own, depth_cells), halo, near)
    parts = lax.all_to_all(parts, "gz", 0, 0, axis_index_groups=runs)
    parts = merge(parts, far, False)
    parts = lax.all_to_all(parts, "gz", 0, 0, axis_index_groups=strides)
    parts = merge(parts, near, True)
    return lay(lax.all_to_all(parts, "gz", 0, 0, axis_index_groups=runs))


def solution(mesh):
    return jax.shard_map(
        per_device,
        mesh=mesh,
        in_specs=(P("gz", "gx", "gy"),),
        out_specs=P(None, "gx", "gy"),
        check_vma=False,
    )
```

```python
import functools

import jax
import jax.numpy as jnp
from jax import lax
from jax.experimental import pallas as pl
from jax.experimental.pallas import tpu as pltpu
from jax.sharding import PartitionSpec as P

E = 2.718281828459045
VMEM = pltpu.VMEM


def whole():
    return pl.BlockSpec(memory_space=VMEM)


def faces_kernel(steps, v_ref, own_ref, pair_ref, rest_ref, xlo_ref, xhi_ref, y_ref, sems):
    nz, nx, ny = v_ref.shape
    deep = nz // steps
    copies = []
    for i in range(steps):
        planes = slice(i * deep, (i + 1) * deep)
        copies.append(pltpu.make_async_copy(v_ref.at[planes], own_ref.at[planes], sems.at[i]))
        copies[-1].start()
    lane_pair = lax.broadcasted_iota(jnp.int32, (8, ny), 1) // 2
    for i in range(steps):
        copies[i].wait()
        for row in range(0, nx, 8):
            packed = jnp.zeros((8, ny), jnp.float32) if i == 0 else y_ref[row : row + 8, :]
            for z in range(i * deep, (i + 1) * deep):
                turned = pltpu.roll(own_ref[z, row : row + 8, :], 2 * z + 1, 1)
                packed = jnp.where(lane_pair == z, turned, packed)
            y_ref[row : row + 8, :] = packed
        for z in range(i * deep, (i + 1) * deep):
            xlo_ref[z : z + 1, :] = own_ref[z, 0:1, :]
            xhi_ref[z : z + 1, :] = own_ref[z, nx - 1 : nx, :]
    odd = lax.rem(lax.axis_index("gz"), 2)
    pair_ref[...] = own_ref[(1 - odd) * (nz - 1)]
    rest_ref[...] = own_ref[odd * (nz - 1)]


def faces(volume):
    nz, nx, ny = volume.shape
    steps = 4
    plane = jax.ShapeDtypeStruct((nx, ny), jnp.float32)
    row = jax.ShapeDtypeStruct((nz, ny), jnp.float32)
    return pl.pallas_call(
        functools.partial(faces_kernel, steps),
        out_shape=(jax.ShapeDtypeStruct(volume.shape, jnp.float32), plane, plane, row, row, plane),
        in_specs=[pl.BlockSpec(memory_space=pltpu.HBM)],
        out_specs=[whole()] * 6,
        scratch_shapes=[pltpu.SemaphoreType.DMA((steps,))],
        compiler_params=pltpu.CompilerParams(vmem_limit_bytes=8 << 20),
        name="faces",
    )(pltpu.with_memory_space_constraint(volume, pltpu.HBM))


def weigh_kernel(scale, v_ref, red_ref, green_ref, blue_ref, clear_ref):
    nz, nx, ny = v_ref.shape
    height, unroll = 16, 16
    for start in range(0, nx, height):
        rows = slice(start, start + height)

        def group(k, clear):
            for i in range(unroll):
                z = k * unroll + i
                cur = v_ref[z, rows, :]
                grown = jnp.exp(cur)
                thick = grown * scale
                opacity = thick * (1.0 + thick * (-1.0 / 2 + thick * (1.0 / 6 + thick * (-1.0 / 24 + thick * (1.0 / 120)))))
                square = grown * grown
                up = square * E
                low = 1.0 + square * (1.0 / E)
                ratio = 1.0 / ((1.0 + up) * low)
                weight = clear * opacity
                share = weight * ratio
                red_ref[z, rows, :] = share * (up * low)
                green_ref[z, rows, :] = weight * jnp.exp(-cur * cur)
                blue_ref[z, rows, :] = share * (1.0 + up)
                clear = clear - weight
            return clear

        clear_ref[rows, :] = lax.fori_loop(0, nz // unroll, group, jnp.ones((height, ny), jnp.float32))


def weigh(volume, depth_cells):
    nz, nx, ny = volume.shape
    brick = jax.ShapeDtypeStruct(volume.shape, jnp.float32)
    return pl.pallas_call(
        functools.partial(weigh_kernel, 2.0 / depth_cells),
        out_shape=(brick, brick, brick, jax.ShapeDtypeStruct((nx, ny), jnp.float32)),
        in_specs=[whole()],
        out_specs=[whole()] * 4,
        compiler_params=pltpu.CompilerParams(vmem_limit_bytes=12 << 20),
        cost_estimate=pl.CostEstimate(flops=30 * nz * nx * ny, bytes_accessed=16 * nz * nx * ny, transcendentals=3 * nz * nx * ny),
        name="weigh",
    )(volume)


def shade_kernel(v_ref, red_ref, green_ref, blue_ref, clear_ref, zpair_ref, zrest_ref, xlo_ref, xhi_ref, ypair_ref, yrest_ref, out_ref):
    odd_z = lax.rem(lax.axis_index("gz"), 2) == 1
    odd_y = lax.rem(lax.axis_index("gy"), 2) == 1
    nz, nx, ny = v_ref.shape
    pieces = out_ref.shape[0]
    height, unroll = nx // pieces, 16
    col = lax.broadcasted_iota(jnp.int32, (height, ny), 1)
    line = lax.broadcasted_iota(jnp.int32, (height, ny), 0)
    odd = col % 2 == 1
    for block in range(pieces):
        start = block * height
        rows = slice(start, start + height)
        pair, rest = ypair_ref[rows, :], yrest_ref[rows, :]
        before, after = jnp.where(odd_y, pair, rest), jnp.where(odd_y, rest, pair)
        edge = jnp.where(odd, pltpu.roll(before, 1, 1), pltpu.roll(after, ny - 1, 1))
        front = jnp.where(odd_z, zpair_ref[rows, :], zrest_ref[rows, :])
        back = jnp.where(odd_z, zrest_ref[rows, :], zpair_ref[rows, :])

        def step(z, prev, cur, new, sums):
            if block == 0:
                above = jnp.where(line == 0, xlo_ref[pl.ds(z, 1), :], pltpu.roll(cur, 1, 0))
            else:
                above = v_ref[z, start - 1 : start - 1 + height, :]
            if block == pieces - 1:
                below = jnp.where(line == height - 1, xhi_ref[pl.ds(z, 1), :], pltpu.roll(cur, height - 1, 0))
            else:
                below = v_ref[z, start + 1 : start + 1 + height, :]
            outer = pltpu.roll(edge, ny - 1 - 2 * z, 1)
            left = jnp.where(col == 0, outer, pltpu.roll(cur, 1, 1))
            right = jnp.where(col == ny - 1, outer, pltpu.roll(cur, ny - 1, 1))
            dz = new - prev
            dx = below - above
            dy = right - left
            facing = jnp.abs(2.0 * (dz + dy) + dx)
            shading = 0.2 + (2.0 / 3.0) * facing * lax.rsqrt(dz * dz + dx * dx + dy * dy + 4.0)
            return tuple(s + ref[z, rows, :] * shading for s, ref in zip(sums, (red_ref, green_ref, blue_ref)))

        def group(k, carry):
            prev, cur, sums = carry
            for i in range(unroll):
                z = k * unroll + i
                new = v_ref[z + 1, rows, :]
                sums = step(z, prev, cur, new, sums)
                prev, cur = cur, new
            return prev, cur, sums

        zero = jnp.zeros((height, ny), jnp.float32)
        prev, cur, sums = lax.fori_loop(0, nz // unroll - 1, group, (front, v_ref[0, rows, :], (zero,) * 3))
        for z in range(nz - unroll, nz):
            new = v_ref[z + 1, rows, :] if z + 1 < nz else back
            sums = step(z, prev, cur, new, sums)
            prev, cur = cur, new
        for c, value in enumerate((*sums, clear_ref[rows, :])):
            out_ref[block, c * height : (c + 1) * height, :] = value


def shade(volume, weights, halo, pieces):
    nz, nx, ny = volume.shape
    return pl.pallas_call(
        shade_kernel,
        out_shape=jax.ShapeDtypeStruct((pieces, 4 * nx // pieces, ny), jnp.float32),
        in_specs=[whole()] * 11,
        out_specs=whole(),
        compiler_params=pltpu.CompilerParams(vmem_limit_bytes=12 << 20),
        name="shade",
    )(volume, *weights, *halo)


def merge_kernel(final, parts_ref, out_ref):
    count, rows, ny = parts_ref.shape
    part = rows // 4
    clear = parts_ref[0, 3 * part :, :]
    total = [parts_ref[0, c * part : (c + 1) * part, :] for c in range(3)]
    for k in range(1, count):
        for c in range(3):
            total[c] = total[c] + clear * parts_ref[k, c * part : (c + 1) * part, :]
        clear = clear * parts_ref[k, 3 * part :, :]
    total.append(1.0 - clear if final else clear)
    for k in range(out_ref.shape[0]):
        for c in range(4):
            out_ref[k, c * part : (c + 1) * part, :] = total[c]


def merge(parts, copies, final):
    _, rows, ny = parts.shape
    return pl.pallas_call(
        functools.partial(merge_kernel, final),
        out_shape=jax.ShapeDtypeStruct((copies, rows, ny), jnp.float32),
        in_specs=[whole()],
        out_specs=whole(),
        compiler_params=pltpu.CompilerParams(vmem_limit_bytes=8 << 20),
        name="merge",
    )(parts)


def lay_kernel(parts_ref, out_ref):
    count, rows, ny = parts_ref.shape
    part = rows // 4
    for k in range(count):
        for c in range(4):
            out_ref[c, k * part : (k + 1) * part, :] = parts_ref[k, c * part : (c + 1) * part, :]


def lay(parts):
    count, rows, ny = parts.shape
    return pl.pallas_call(
        lay_kernel,
        out_shape=jax.ShapeDtypeStruct((4, count * rows // 4, ny), jnp.float32),
        in_specs=[whole()],
        out_specs=whole(),
        compiler_params=pltpu.CompilerParams(vmem_limit_bytes=8 << 20),
        name="lay",
    )(parts)


def shift(array, axis, upward):
    devices = lax.axis_size(axis)
    pairs = [(i, i + 1) if upward else (i + 1, i) for i in range(devices - 1)]
    return lax.ppermute(array, axis, pairs)


def swap(array, axis, first):
    lower = range(first, lax.axis_size(axis) - 1, 2)
    return lax.ppermute(array, axis, [p for i in lower for p in ((i, i + 1), (i + 1, i))])


def per_device(volume):
    bricks = lax.axis_size("gz")
    depth_cells = volume.shape[0] * bricks
    own, zpair, zrest, xlo, xhi, y = faces(volume)
    zrest = swap(zrest, "gz", 1)
    zpair = swap(zpair, "gz", 0)
    ypair = swap(y, "gy", 0)
    yrest = swap(y, "gy", 1)
    above = shift(xhi, "gx", True)
    xlo, zrest = lax.optimization_barrier((xlo, zrest))
    below = shift(xlo, "gx", False)
    halo = (zpair, zrest, above, below, ypair, yrest)
    near = max(n for n in (1, 2, 4, 8) if bricks % n == 0)
    far = bricks // near
    runs = [[g * near + i for i in range(near)] for g in range(far)]
    strides = [[g * near + i for g in range(far)] for i in range(near)]
    parts = shade(own, weigh(own, depth_cells), halo, near)
    parts = lax.all_to_all(parts, "gz", 0, 0, axis_index_groups=runs)
    parts = merge(parts, far, False)
    parts = lax.all_to_all(parts, "gz", 0, 0, axis_index_groups=strides)
    parts = merge(parts, near, True)
    return lay(lax.all_to_all(parts, "gz", 0, 0, axis_index_groups=runs))


def solution(mesh):
    return jax.shard_map(
        per_device,
        mesh=mesh,
        in_specs=(P("gz", "gx", "gy"),),
        out_specs=P(None, "gx", "gy"),
        check_vma=False,
    )
```

```python
import functools

import jax
import jax.numpy as jnp
from jax import lax
from jax.experimental import pallas as pl
from jax.experimental.pallas import tpu as pltpu
from jax.sharding import PartitionSpec as P

E = 2.718281828459045
VMEM = pltpu.VMEM


def whole():
    return pl.BlockSpec(memory_space=VMEM)


def faces_kernel(steps, v_ref, own_ref, pair_ref, rest_ref, xlo_ref, xhi_ref, y_ref, sems):
    nz, nx, ny = v_ref.shape
    deep = nz // steps
    copies = []
    for i in range(steps):
        planes = slice(i * deep, (i + 1) * deep)
        copies.append(pltpu.make_async_copy(v_ref.at[planes], own_ref.at[planes], sems.at[i]))
        copies[-1].start()
    lane_pair = lax.broadcasted_iota(jnp.int32, (8, ny), 1) // 2
    for i in range(steps):
        copies[i].wait()
        for row in range(0, nx, 8):
            packed = jnp.zeros((8, ny), jnp.float32) if i == 0 else y_ref[row : row + 8, :]
            for z in range(i * deep, (i + 1) * deep):
                turned = pltpu.roll(own_ref[z, row : row + 8, :], 2 * z + 1, 1)
                packed = jnp.where(lane_pair == z, turned, packed)
            y_ref[row : row + 8, :] = packed
        for z in range(i * deep, (i + 1) * deep):
            xlo_ref[z : z + 1, :] = own_ref[z, 0:1, :]
            xhi_ref[z : z + 1, :] = own_ref[z, nx - 1 : nx, :]
    odd = lax.rem(lax.axis_index("gz"), 2)
    pair_ref[...] = own_ref[(1 - odd) * (nz - 1)]
    rest_ref[...] = own_ref[odd * (nz - 1)]


def faces(volume):
    nz, nx, ny = volume.shape
    steps = 4
    plane = jax.ShapeDtypeStruct((nx, ny), jnp.float32)
    row = jax.ShapeDtypeStruct((nz, ny), jnp.float32)
    return pl.pallas_call(
        functools.partial(faces_kernel, steps),
        out_shape=(jax.ShapeDtypeStruct(volume.shape, jnp.float32), plane, plane, row, row, plane),
        in_specs=[pl.BlockSpec(memory_space=pltpu.HBM)],
        out_specs=[whole()] * 6,
        scratch_shapes=[pltpu.SemaphoreType.DMA((steps,))],
        compiler_params=pltpu.CompilerParams(vmem_limit_bytes=8 << 20),
        name="faces",
    )(pltpu.with_memory_space_constraint(volume, pltpu.HBM))


def weigh_kernel(scale, v_ref, red_ref, green_ref, blue_ref, clear_ref):
    nz, nx, ny = v_ref.shape
    height, unroll = 16, 16
    for start in range(0, nx, height):
        rows = slice(start, start + height)

        def group(k, clear):
            for i in range(unroll):
                z = k * unroll + i
                cur = v_ref[z, rows, :]
                grown = jnp.exp(cur)
                thick = grown * scale
                opacity = thick * (1.0 + thick * (-1.0 / 2 + thick * (1.0 / 6 + thick * (-1.0 / 24 + thick * (1.0 / 120)))))
                square = grown * grown
                up = square * E
                low = 1.0 + square * (1.0 / E)
                ratio = 1.0 / ((1.0 + up) * low)
                weight = clear * opacity
                share = weight * ratio
                red_ref[z, rows, :] = share * (up * low)
                green_ref[z, rows, :] = weight * jnp.exp(-cur * cur)
                blue_ref[z, rows, :] = share * (1.0 + up)
                clear = clear - weight
            return clear

        clear_ref[rows, :] = lax.fori_loop(0, nz // unroll, group, jnp.ones((height, ny), jnp.float32))


def weigh(volume, depth_cells):
    nz, nx, ny = volume.shape
    brick = jax.ShapeDtypeStruct(volume.shape, jnp.float32)
    return pl.pallas_call(
        functools.partial(weigh_kernel, 2.0 / depth_cells),
        out_shape=(brick, brick, brick, jax.ShapeDtypeStruct((nx, ny), jnp.float32)),
        in_specs=[whole()],
        out_specs=[whole()] * 4,
        compiler_params=pltpu.CompilerParams(vmem_limit_bytes=12 << 20),
        cost_estimate=pl.CostEstimate(flops=30 * nz * nx * ny, bytes_accessed=16 * nz * nx * ny, transcendentals=3 * nz * nx * ny),
        name="weigh",
    )(volume)


def shade_kernel(v_ref, red_ref, green_ref, blue_ref, clear_ref, zpair_ref, zrest_ref, xlo_ref, xhi_ref, ypair_ref, yrest_ref, out_ref):
    odd_z = lax.rem(lax.axis_index("gz"), 2) == 1
    odd_y = lax.rem(lax.axis_index("gy"), 2) == 1
    nz, nx, ny = v_ref.shape
    pieces = out_ref.shape[0]
    height, unroll = 16, 16
    tall = nx // pieces
    col = lax.broadcasted_iota(jnp.int32, (height, ny), 1)
    line = lax.broadcasted_iota(jnp.int32, (height, ny), 0)
    odd = col % 2 == 1
    for block in range(nx // height):
        start = block * height
        rows = slice(start, start + height)
        pair, rest = ypair_ref[rows, :], yrest_ref[rows, :]
        before, after = jnp.where(odd_y, pair, rest), jnp.where(odd_y, rest, pair)
        edge = jnp.where(odd, pltpu.roll(before, 1, 1), pltpu.roll(after, ny - 1, 1))
        front = jnp.where(odd_z, zpair_ref[rows, :], zrest_ref[rows, :])
        back = jnp.where(odd_z, zrest_ref[rows, :], zpair_ref[rows, :])

        def step(z, prev, cur, new, sums):
            if block == 0:
                above = jnp.where(line == 0, xlo_ref[pl.ds(z, 1), :], pltpu.roll(cur, 1, 0))
            else:
                above = v_ref[z, start - 1 : start - 1 + height, :]
            if start + height == nx:
                below = jnp.where(line == height - 1, xhi_ref[pl.ds(z, 1), :], pltpu.roll(cur, height - 1, 0))
            else:
                below = v_ref[z, start + 1 : start + 1 + height, :]
            outer = pltpu.roll(edge, ny - 1 - 2 * z, 1)
            left = jnp.where(col == 0, outer, pltpu.roll(cur, 1, 1))
            right = jnp.where(col == ny - 1, outer, pltpu.roll(cur, ny - 1, 1))
            dz = new - prev
            dx = below - above
            dy = right - left
            facing = jnp.abs(2.0 * (dz + dy) + dx)
            shading = 0.2 + (2.0 / 3.0) * facing * lax.rsqrt(dz * dz + dx * dx + dy * dy + 4.0)
            return tuple(s + ref[z, rows, :] * shading for s, ref in zip(sums, (red_ref, green_ref, blue_ref)))

        def group(k, carry):
            prev, cur, sums = carry
            for i in range(unroll):
                z = k * unroll + i
                new = v_ref[z + 1, rows, :]
                sums = step(z, prev, cur, new, sums)
                prev, cur = cur, new
            return prev, cur, sums

        zero = jnp.zeros((height, ny), jnp.float32)
        prev, cur, sums = lax.fori_loop(0, nz // unroll - 1, group, (front, v_ref[0, rows, :], (zero,) * 3))
        for z in range(nz - unroll, nz):
            new = v_ref[z + 1, rows, :] if z + 1 < nz else back
            sums = step(z, prev, cur, new, sums)
            prev, cur = cur, new
        for c, value in enumerate((*sums, clear_ref[rows, :])):
            place = c * tall + start % tall
            out_ref[start // tall, place : place + height, :] = value


def shade(volume, weights, halo, pieces):
    nz, nx, ny = volume.shape
    return pl.pallas_call(
        shade_kernel,
        out_shape=jax.ShapeDtypeStruct((pieces, 4 * nx // pieces, ny), jnp.float32),
        in_specs=[whole()] * 11,
        out_specs=whole(),
        compiler_params=pltpu.CompilerParams(vmem_limit_bytes=12 << 20),
        name="shade",
    )(volume, *weights, *halo)


def composite(parts_ref):
    count, rows, _ = parts_ref.shape
    part = rows // 4
    clear = parts_ref[0, 3 * part :, :]
    total = [parts_ref[0, c * part : (c + 1) * part, :] for c in range(3)]
    for k in range(1, count):
        for c in range(3):
            total[c] = total[c] + clear * parts_ref[k, c * part : (c + 1) * part, :]
        clear = clear * parts_ref[k, 3 * part :, :]
    return total, clear


def cut_kernel(parts_ref, out_ref):
    total, clear = composite(parts_ref)
    part = out_ref.shape[1] // 4
    for k in range(out_ref.shape[0]):
        for c, value in enumerate((*total, clear)):
            out_ref[k, c * part : (c + 1) * part, :] = value[k * part : (k + 1) * part, :]


def final_kernel(parts_ref, out_ref):
    total, clear = composite(parts_ref)
    part = out_ref.shape[1] // 4
    for k in range(out_ref.shape[0]):
        for c, value in enumerate((*total, 1.0 - clear)):
            out_ref[k, c * part : (c + 1) * part, :] = value


def repeat_kernel(parts_ref, out_ref):
    for k in range(out_ref.shape[0]):
        out_ref[k] = parts_ref[...]


def lay_kernel(parts_ref, out_ref):
    runs, count, rows, _ = parts_ref.shape
    part = rows // 4
    for r in range(runs):
        for k in range(count):
            for c in range(4):
                row = (r * count + k) * part
                out_ref[c, row : row + part, :] = parts_ref[r, k, c * part : (c + 1) * part, :]


def small(kernel, shape, parts):
    return pl.pallas_call(
        kernel,
        out_shape=jax.ShapeDtypeStruct(shape, jnp.float32),
        in_specs=[whole()],
        out_specs=whole(),
        compiler_params=pltpu.CompilerParams(vmem_limit_bytes=8 << 20),
        name=kernel.__name__,
    )(parts)


def shift(array, axis, upward):
    devices = lax.axis_size(axis)
    pairs = [(i, i + 1) if upward else (i + 1, i) for i in range(devices - 1)]
    return lax.ppermute(array, axis, pairs)


def swap(array, axis, first):
    lower = range(first, lax.axis_size(axis) - 1, 2)
    return lax.ppermute(array, axis, [p for i in lower for p in ((i, i + 1), (i + 1, i))])


def per_device(volume):
    bricks = lax.axis_size("gz")
    depth_cells = volume.shape[0] * bricks
    own, zpair, zrest, xlo, xhi, y = faces(volume)
    zrest = swap(zrest, "gz", 1)
    zpair = swap(zpair, "gz", 0)
    ypair = swap(y, "gy", 0)
    yrest = swap(y, "gy", 1)
    above = shift(xhi, "gx", True)
    xlo, zrest = lax.optimization_barrier((xlo, zrest))
    below = shift(xlo, "gx", False)
    halo = (zpair, zrest, above, below, ypair, yrest)
    nx, ny = volume.shape[1:]
    near = 4
    far = bricks // near
    runs = [[g * near + i for i in range(near)] for g in range(far)]
    strides = [[g * near + i for g in range(far)] for i in range(near)]
    piece = (far, 4 * nx // bricks, ny)
    parts = shade(own, weigh(own, depth_cells), halo, near)
    parts = lax.all_to_all(parts, "gz", 0, 0, axis_index_groups=runs)
    parts = small(cut_kernel, piece, parts)
    parts = lax.all_to_all(parts, "gz", 0, 0, axis_index_groups=strides)
    parts = small(final_kernel, piece, parts)
    parts = lax.all_to_all(parts, "gz", 0, 0, axis_index_groups=strides)
    parts = small(repeat_kernel, (near, *piece), parts)
    parts = lax.all_to_all(parts, "gz", 0, 0, axis_index_groups=runs)
    return small(lay_kernel, (4, nx, ny), parts)


def solution(mesh):
    return jax.shard_map(
        per_device,
        mesh=mesh,
        in_specs=(P("gz", "gx", "gy"),),
        out_specs=P(None, "gx", "gy"),
        check_vma=False,
    )
```
